32 devices in a mesh: occ: 8 (over z, y), aux: 4 (over x, core).
Axes of the slice: x: 2, y: 2, z: 4, core: 2. Of those that a mesh axis runs over, the one named last changes fastest.
Arguments:
- b_alpha: bfloat16 [16, 512, 1536], P('occ', None, 'aux'), may hold values from -0.95703125 to 0.95703125
- b_beta: bfloat16 [16, 512, 1536], P('occ', None, 'aux'), may hold values from -0.95703125 to 0.95703125
- eps_occ_alpha: float32 [16], replicated, may hold values from -3 to -0.3
- eps_occ_beta: float32 [16], replicated, may hold values from -3 to -0.3
- eps_vir_alpha: float32 [512], replicated, may hold values from 0.2 to 4
- eps_vir_beta: float32 [512], replicated, may hold values from 0.2 to 4
- row_orbital: int32 [16], replicated, may hold values from 0 to 15, as said below
- pair_list: int32 [4, 8, 2], replicated, may hold values from 0 to 15, as said below
- live_mask: int32 [4, 8], replicated, may hold values 0 or 1
Outputs:
- gamma_alpha: float32 [16, 512, 1536], P('occ', None, 'aux')
- gamma_beta: float32 [16, 512, 1536], P('occ', None, 'aux')
The draws below stay inside these ranges and needn't reach their ends.
Inputs may be any that keep to these rules, and one draw needn't show every extreme that they name: A permutation: stored row r of b_alpha, b_beta and the outputs belongs to occupied orbital row_orbital[r]. `pair_list`: for slot s and worker w the entry (i, j) has r(i) among the stored rows w * 2 to (w + 1) * 2 - 1 and r(j) among the stored rows of worker (w - d) mod 8, where d = 1 + s * (8 // 4) and r is the inverse of row_orbital.
All inputs are finite; a program needn't handle non-finite values.
Results may differ from the reference program's by a relative error of at most 0.01.
Values may be sent and summed in bfloat16 or wider, within the bound.
A program may use at most 64 MiB of HBM per device.

```python
import jax
import jax.numpy as jnp
from jax import lax

NVIR = 512
NAUX = 1536
OCC_DEV = 2
BATCHES = 2
ROUNDS = 2
OCC = 16
SLOTS = 4
N_OCC = 8
N_AUX = 4


def orbital_map(key):
    return jax.random.permutation(jax.random.fold_in(key, 11), OCC).astype(jnp.int32)


def draw_row_orbital(key, part):
    return orbital_map(key)


def draw_pair_list(key, part):
    mapping = orbital_map(key)
    workers = OCC // OCC_DEV
    slot_count = BATCHES * ROUNDS
    distances = 1 + jnp.arange(slot_count, dtype=jnp.int32) * (workers // slot_count)
    owners = jnp.arange(workers, dtype=jnp.int32)
    pick_i = jax.random.randint(jax.random.fold_in(key, 23), (slot_count, workers), 0, OCC_DEV)
    pick_j = jax.random.randint(jax.random.fold_in(key, 29), (slot_count, workers), 0, OCC_DEV)
    rows_i = owners[None, :] * OCC_DEV + pick_i
    rows_j = jnp.mod(owners[None, :] - distances[:, None], workers) * OCC_DEV + pick_j
    return jnp.stack([mapping[rows_i], mapping[rows_j]], axis=-1).astype(jnp.int32)


def plant(values, stream_key, smallest, top_value):
    place = [jax.random.randint(jax.random.fold_in(stream_key, axis), (), 0, length) for axis, length in enumerate(values.shape)]
    widest = values.shape.index(max(values.shape))
    next_to = place[:widest] + [(place[widest] + 1) % values.shape[widest]] + place[widest + 1:]
    return values.at[tuple(place)].set(smallest).at[tuple(next_to)].set(top_value)


def level_of(own_key, extent, cuts, least, largest):
    gain, own = 1.0, jax.random.fold_in(own_key, 6)
    for dim, shards_of in cuts:
        draws = jnp.exp(jax.random.uniform(jax.random.fold_in(own, dim), (shards_of,), jnp.float32, least / len(cuts), largest / len(cuts)))
        gain = gain * jnp.repeat(draws, extent[dim] // shards_of).reshape([-1 if axis == dim else 1 for axis in range(len(extent))])
    return gain


def noise(rng, shape, spread, bound, shards=(), kind=jnp.bfloat16):
    level = level_of(rng, shape, shards, -0.22, 0.18) if shards else 1.0
    drawn = jax.random.normal(rng, shape, jnp.float32) * spread * level
    return jnp.minimum(jnp.maximum(drawn, -bound), bound).astype(kind)


def setup_inputs(seed: int = 0) -> dict:
    streams_of = jax.random.split(jax.random.key(seed), 10)
    b_alpha = noise(streams_of[0], (OCC, NVIR, NAUX), 0.16, 0.95703125, ((0, 8), (2, 4)))
    b_beta = noise(streams_of[1], (OCC, NVIR, NAUX), 0.16, 0.95703125, ((0, 8), (2, 4)))
    eps_occ_alpha = jnp.clip(jax.random.uniform(streams_of[2], (OCC,), jnp.float32, -3.0, -0.3), -3.0, -0.3)
    eps_occ_beta = jnp.clip(jax.random.uniform(streams_of[3], (OCC,), jnp.float32, -3.0, -0.3), -3.0, -0.3)
    eps_vir_alpha = jnp.clip(jax.random.uniform(streams_of[4], (NVIR,), jnp.float32, 0.2, 4.0), 0.2, 4.0)
    eps_vir_beta = jnp.clip(jax.random.uniform(streams_of[5], (NVIR,), jnp.float32, 0.2, 4.0), 0.2, 4.0)
    row_orbital = draw_row_orbital(jax.random.fold_in(streams_of[9], 71), 0)
    pair_list = draw_pair_list(jax.random.fold_in(streams_of[9], 71), 0)
    live_mask = plant((jax.random.randint(streams_of[8], (SLOTS, N_OCC), 0, 4) < 3).astype(jnp.int32), jax.random.fold_in(streams_of[8], 1), 0, 1)
    return {"b_alpha": b_alpha, "b_beta": b_beta, "eps_occ_alpha": eps_occ_alpha, "eps_occ_beta": eps_occ_beta, "eps_vir_alpha": eps_vir_alpha, "eps_vir_beta": eps_vir_beta, "row_orbital": row_orbital, "pair_list": pair_list, "live_mask": live_mask}


def add_row(totals, row_index, row_term):
    current = lax.dynamic_index_in_dim(totals, row_index, 0, keepdims=False)
    return lax.dynamic_update_index_in_dim(totals, current + row_term, row_index, 0)


def reference(b_alpha, b_beta, eps_occ_alpha, eps_occ_beta, eps_vir_alpha, eps_vir_beta, row_orbital, pair_list, live_mask):
    places = jnp.arange(OCC, dtype=jnp.int32)
    inverse = jnp.zeros((OCC,), jnp.int32).at[row_orbital].set(places)
    alpha_full = b_alpha.astype(jnp.float32)
    beta_full = b_beta.astype(jnp.float32)
    flat_pairs = pair_list.reshape(-1, 2).astype(jnp.int32)
    flat_live = live_mask.reshape(-1).astype(jnp.float32)

    def advance(state_pair, item):
        gamma_alpha, gamma_beta = state_pair
        orbitals, live_flag = item
        row_i = inverse[orbitals[0]].astype(jnp.int32)
        row_j = inverse[orbitals[1]].astype(jnp.int32)
        block_i = lax.dynamic_index_in_dim(alpha_full, row_i, 0, keepdims=False)
        block_j = lax.dynamic_index_in_dim(beta_full, row_j, 0, keepdims=False)
        split_i = block_i.reshape(NVIR, N_AUX, NAUX // N_AUX)
        split_j = block_j.reshape(NVIR, N_AUX, NAUX // N_AUX)
        partials = jnp.einsum("akp,bkp->kab", split_i, split_j, precision=lax.Precision.HIGHEST)
        rounded = lax.optimization_barrier(partials.astype(jnp.bfloat16))
        integrals = jnp.sum(rounded.astype(jnp.float32), axis=0)
        energy_gap = eps_vir_alpha[:, None] + eps_vir_beta[None, :] - eps_occ_alpha[orbitals[0]] - eps_occ_beta[orbitals[1]]
        amplitude = (live_flag * integrals / energy_gap).astype(jnp.bfloat16)
        amplitude = lax.optimization_barrier(amplitude).astype(jnp.float32)
        term_alpha = jnp.dot(amplitude, block_j, precision=lax.Precision.HIGHEST)
        term_beta = jnp.dot(amplitude.T, block_i, precision=lax.Precision.HIGHEST)
        gamma_alpha = add_row(gamma_alpha, row_i, term_alpha)
        gamma_beta = add_row(gamma_beta, row_j, term_beta)
        return (gamma_alpha, gamma_beta), jnp.float32(0.0)

    zeros_full = jnp.zeros((OCC, NVIR, NAUX), jnp.float32)
    finals, unused = lax.scan(advance, (zeros_full, zeros_full), (flat_pairs, flat_live))
    return finals[0], finals[1]
```

```python
import functools

import jax
import jax.numpy as jnp
from jax import lax
from jax.experimental import pallas as pl
from jax.experimental.pallas import tpu as pltpu
from jax.sharding import PartitionSpec as P

MESH = pl.DeviceIdType.MESH


def kernel(
    workers,
    parts,
    slots,
    b_alpha,
    b_beta,
    eps_vir_alpha,
    eps_vir_beta,
    eps_occ_alpha,
    eps_occ_beta,
    row_orbital,
    pair_list,
    live_mask,
    gamma_alpha,
    gamma_beta,
    send_block,
    block_j,
    part_send,
    part_recv,
    amp,
    term_send,
    term_recv,
    fetch_sems,
    part_sems,
    amp_sems,
    term_sems,
):
    rows, nvir, cols = b_alpha.shape
    quarter = nvir // parts
    worker = lax.axis_index("occ")
    me = lax.axis_index("aux")
    distances = [1 + s * (workers // slots) for s in range(slots)]
    ahead = [lax.rem(worker + d, workers) for d in distances]
    behind = [lax.rem(worker + workers - d, workers) for d in distances]
    peers = [lax.rem(me + k, parts) for k in range(1, parts)]

    barrier = pltpu.get_barrier_semaphore()
    for target in ahead + behind:
        pl.semaphore_signal(barrier, inc=1, device_id={"occ": target}, device_id_type=MESH)
    for peer in peers:
        pl.semaphore_signal(barrier, inc=1, device_id={"aux": peer}, device_id_type=MESH)

    def local_row(label):
        found = jnp.int32(0)
        for r in range(rows):
            found = jnp.where(row_orbital[worker * rows + r] == label, r, found)
        return found

    row_i = [local_row(pair_list[s, worker, 0]) for s in range(slots)]
    row_out = [local_row(pair_list[s, ahead[s], 1]) for s in range(slots)]
    for s in range(slots):
        send_block[s] = b_beta[row_out[s]]
    pl.semaphore_wait(barrier, 2 * slots + parts - 1)

    def remote(src, dst, sems, index, where):
        return pltpu.make_async_remote_copy(
            src_ref=src,
            dst_ref=dst,
            send_sem=sems.at[(0,) + index],
            recv_sem=sems.at[(1,) + index],
            device_id=where,
            device_id_type=MESH,
        )

    fetches = [
        remote(send_block.at[s], block_j.at[s], fetch_sems, (s,), {"occ": ahead[s]})
        for s in range(slots)
    ]
    part_copies = [
        [
            remote(part_send.at[s, peers[k]], part_recv.at[s, k], part_sems, (s, k), {"aux": peers[k]})
            for k in range(parts - 1)
        ]
        for s in range(slots)
    ]
    amp_copies = [
        [
            remote(amp.at[s, me], amp.at[s, me], amp_sems, (s, k), {"aux": peers[k]})
            for k in range(parts - 1)
        ]
        for s in range(slots)
    ]
    returns = [
        remote(term_send.at[s], term_recv.at[s], term_sems, (s,), {"occ": behind[s]})
        for s in range(slots)
    ]
    for fetch in fetches:
        fetch.start()

    vir_row = eps_vir_alpha[pl.ds(me, 1), :]
    vir_gap = jnp.broadcast_to(vir_row, (quarter, quarter)).T[:, :1] + eps_vir_beta[...]

    def add_rows(totals, first, picked, term):
        for r in range(rows):
            share = jnp.where(picked == r, term, 0.0)
            totals[r] = share if first else totals[r] + share

    def sums(s):
        fetches[s].wait_recv()
        partial = lax.dot_general(
            b_alpha[row_i[s]],
            block_j[s],
            (((1,), (1,)), ((), ())),
            preferred_element_type=jnp.float32,
        )
        part_send[s] = partial.astype(jnp.bfloat16).reshape(parts, quarter, nvir)
        for copy in part_copies[s]:
            copy.start()

    def amplitude(s):
        total = part_send[s, me].astype(jnp.float32)
        for k in range(parts - 1):
            part_copies[s][k].wait_recv()
            total = total + part_recv[s, k].astype(jnp.float32)
        occ = eps_occ_alpha[pair_list[s, worker, 0]]
        occ_beta = eps_occ_beta[pair_list[s, worker, 1]]
        live = live_mask[s, worker].astype(jnp.float32)
        amp[s, me] = (live * total / (vir_gap - occ - occ_beta)).astype(jnp.bfloat16)
        for copy in amp_copies[s]:
            copy.start()

    def terms(s):
        for copy in amp_copies[s]:
            copy.wait_recv()
        whole = amp[s].reshape(nvir, nvir)
        term_send[s] = lax.dot_general(
            whole,
            b_alpha[row_i[s]],
            (((0,), (0,)), ((), ())),
            preferred_element_type=jnp.float32,
        ).astype(jnp.bfloat16)
        returns[s].start()
        add_rows(
            gamma_alpha,
            s == 0,
            row_i[s],
            jnp.dot(whole, block_j[s], preferred_element_type=jnp.float32),
        )

    def returned(s):
        returns[s].wait_recv()
        add_rows(gamma_beta, s == 0, row_out[s], term_recv[s].astype(jnp.float32))

    for s in range(slots):
        sums(s)
        if s >= 1:
            terms(s - 1)
        amplitude(s)
    terms(slots - 1)
    for s in range(slots):
        returned(s)
    for s in range(slots):
        fetches[s].wait_send()
        returns[s].wait_send()
        for copy in part_copies[s] + amp_copies[s]:
            copy.wait_send()


def solution(mesh):
    workers, parts = mesh.shape["occ"], mesh.shape["aux"]

    def shards(
        b_alpha,
        b_beta,
        eps_occ_alpha,
        eps_occ_beta,
        eps_vir_alpha,
        eps_vir_beta,
        row_orbital,
        pair_list,
        live_mask,
    ):
        rows, nvir, cols = b_alpha.shape
        slots = pair_list.shape[0]
        quarter = nvir // parts
        vmem = pl.BlockSpec(memory_space=pltpu.VMEM)
        smem = pl.BlockSpec(memory_space=pltpu.SMEM)
        gamma = jax.ShapeDtypeStruct((rows, nvir, cols), jnp.float32)
        block = pltpu.VMEM((slots, nvir, cols), jnp.bfloat16)
        return pl.pallas_call(
            functools.partial(kernel, workers, parts, slots),
            out_shape=(gamma, gamma),
            in_specs=[vmem] * 4 + [smem] * 5,
            out_specs=(vmem, vmem),
            scratch_shapes=[
                block,
                block,
                pltpu.VMEM((slots, parts, quarter, nvir), jnp.bfloat16),
                pltpu.VMEM((slots, parts - 1, quarter, nvir), jnp.bfloat16),
                pltpu.VMEM((slots, parts, quarter, nvir), jnp.bfloat16),
                block,
                block,
                pltpu.SemaphoreType.DMA((2, slots)),
                pltpu.SemaphoreType.DMA((2, slots, parts - 1)),
                pltpu.SemaphoreType.DMA((2, slots, parts - 1)),
                pltpu.SemaphoreType.DMA((2, slots)),
            ],
            compiler_params=pltpu.CompilerParams(
                collective_id=0, has_side_effects=True, vmem_limit_bytes=48 * 1024 * 1024
            ),
        )(
            b_alpha,
            b_beta,
            eps_vir_alpha.reshape(parts, quarter),
            eps_vir_beta.reshape(1, nvir),
            eps_occ_alpha,
            eps_occ_beta,
            row_orbital,
            pair_list,
            live_mask,
        )

    placed = (P("occ", None, "aux"), P("occ", None, "aux"), P(), P(), P(), P(), P(), P(), P())
    return jax.shard_map(
        shards,
        mesh=mesh,
        in_specs=placed,
        out_specs=(P("occ", None, "aux"), P("occ", None, "aux")),
        check_vma=False,
    )
```

```python
import functools

import jax
import jax.numpy as jnp
from jax import lax
from jax.experimental import pallas as pl
from jax.experimental.pallas import tpu as pltpu
from jax.sharding import PartitionSpec as P

MESH = pl.DeviceIdType.MESH


def kernel(
    workers,
    parts,
    slots,
    b_alpha_hbm,
    b_beta_hbm,
    vir_alpha_hbm,
    vir_beta_hbm,
    occ_alpha_hbm,
    occ_beta_hbm,
    row_orbital_hbm,
    pair_list_hbm,
    live_mask_hbm,
    gamma_alpha_hbm,
    gamma_beta_hbm,
    b_alpha,
    b_beta,
    eps_vir_alpha,
    eps_vir_beta,
    eps_occ_alpha,
    eps_occ_beta,
    row_orbital,
    pair_list,
    live_mask,
    gamma_alpha,
    gamma_beta,
    send_block,
    block_j,
    half_send,
    half_recv,
    cross_send,
    cross_recv,
    amp,
    term_send,
    term_recv,
    in_sems,
    out_sems,
    fetch_sems,
    half_sems,
    cross_sems,
    pair_sems,
    far_sems,
    forward_sems,
    term_sems,
):
    rows, nvir, cols = b_alpha.shape
    chips = parts // 2
    quarter = nvir // parts
    worker = lax.axis_index("occ")
    me = lax.axis_index("aux")
    chip, core = me // 2, lax.rem(me, 2)
    partner = me + 1 - 2 * core
    distances = [1 + s * (workers // slots) for s in range(slots)]
    ahead = [lax.rem(worker + d, workers) for d in distances]
    behind = [lax.rem(worker + workers - d, workers) for d in distances]
    others = [lax.rem(chip + k, chips) for k in range(1, chips)]
    sources = [lax.rem(chip + chips - k, chips) for k in range(1, chips)]

    loads = [
        pltpu.make_async_copy(src, dst, in_sems.at[n])
        for n, (src, dst) in enumerate(
            [
                (b_beta_hbm, b_beta),
                (row_orbital_hbm, row_orbital),
                (pair_list_hbm, pair_list),
                (live_mask_hbm, live_mask),
                (occ_alpha_hbm, eps_occ_alpha),
                (occ_beta_hbm, eps_occ_beta),
                (vir_alpha_hbm, eps_vir_alpha),
                (vir_beta_hbm, eps_vir_beta),
                (b_alpha_hbm, b_alpha),
            ]
        )
    ]
    for load in loads:
        load.start()
    barrier = pltpu.get_barrier_semaphore()
    for target in ahead + behind:
        pl.semaphore_signal(barrier, inc=1, device_id={"occ": target}, device_id_type=MESH)
    for peer in [partner] + [other * 2 + core for other in others]:
        pl.semaphore_signal(barrier, inc=1, device_id={"aux": peer}, device_id_type=MESH)
    for load in loads[:3]:
        load.wait()

    def local_row(label):
        found = jnp.int32(0)
        for r in range(rows):
            found = jnp.where(row_orbital[worker * rows + r] == label, r, found)
        return found

    row_i = [local_row(pair_list[s, 0, worker]) for s in range(slots)]
    row_out = [local_row(pair_list[s, 1, ahead[s]]) for s in range(slots)]
    for s in range(slots):
        send_block[s] = b_beta[row_out[s]]
    pl.semaphore_wait(barrier, 2 * slots + chips)

    def remote(src, dst, sems, index, where):
        return pltpu.make_async_remote_copy(
            src_ref=src,
            dst_ref=dst,
            send_sem=sems.at[(0,) + index],
            recv_sem=sems.at[(1,) + index],
            device_id=where,
            device_id_type=MESH,
        )

    each = range(slots)
    hops = range(chips - 1)
    fetches = [
        remote(send_block.at[s], block_j.at[s], fetch_sems, (s,), {"occ": ahead[s]}) for s in each
    ]
    halves = [
        remote(half_send.at[s, 1 - core], half_recv.at[s], half_sems, (s,), {"aux": partner})
        for s in each
    ]
    crosses = [
        [
            remote(
                cross_send.at[s, k], cross_recv.at[s, k], cross_sems, (s, k),
                {"aux": others[k] * 2 + core},
            )
            for k in hops
        ]
        for s in each
    ]
    nears = [
        remote(amp.at[s, core, chip], amp.at[s, core, chip], pair_sems, (s,), {"aux": partner})
        for s in each
    ]
    fars = [
        [
            remote(
                amp.at[s, core, chip], amp.at[s, core, chip], far_sems, (s, k),
                {"aux": others[k] * 2 + core},
            )
            for k in hops
        ]
        for s in each
    ]
    forwards = [
        [
            remote(
                amp.at[s, core, sources[k]], amp.at[s, core, sources[k]], forward_sems, (s, k),
                {"aux": partner},
            )
            for k in hops
        ]
        for s in each
    ]
    returns = [
        remote(term_send.at[s], term_recv.at[s], term_sems, (s,), {"occ": behind[s]}) for s in each
    ]
    for fetch in fetches:
        fetch.start()
    for load in loads[3:]:
        load.wait()

    vir_row = eps_vir_alpha[pl.ds(core * chips + chip, 1), :]
    vir_gap = jnp.broadcast_to(vir_row, (quarter, quarter)).T[:, :1] + eps_vir_beta[...]

    def add_row(totals, first, r, picked, term):
        share = jnp.where(picked == r, term, 0.0)
        totals[r] = share if first else totals[r] + share

    def sums(s):
        fetches[s].wait_recv()
        partial = lax.dot_general(
            b_alpha[row_i[s]],
            block_j[s],
            (((1,), (1,)), ((), ())),
            preferred_element_type=jnp.float32,
        )
        half_send[s] = partial.astype(jnp.bfloat16).reshape(2, chips, quarter, nvir)
        halves[s].start()

    def pair_sum(s, owner):
        return half_send[s, core, owner].astype(jnp.float32) + half_recv[s, owner].astype(jnp.float32)

    def crossing(s):
        halves[s].wait_recv()
        for k in hops:
            cross_send[s, k] = pair_sum(s, others[k]).astype(jnp.bfloat16)
            crosses[s][k].start()

    def amplitude(s):
        total = pair_sum(s, chip)
        for k in hops:
            crosses[s][k].wait_recv()
            total = total + cross_recv[s, k].astype(jnp.float32)
        occ_alpha = eps_occ_alpha[pair_list[s, 0, worker]]
        occ_beta = eps_occ_beta[pair_list[s, 1, worker]]
        live = live_mask[s, worker].astype(jnp.float32)
        amp[s, core, chip] = (live * total / (vir_gap - occ_alpha - occ_beta)).astype(jnp.bfloat16)
        for copy in fars[s]:
            copy.start()
        nears[s].start()

    def forward(s):
        for k in hops:
            fars[s][k].wait_recv()
            forwards[s][k].start()

    def terms(s):
        nears[s].wait_recv()
        for copy in forwards[s]:
            copy.wait_recv()
        whole = amp[s].reshape(nvir, nvir)
        term_send[s] = lax.dot_general(
            whole,
            b_alpha[row_i[s]],
            (((0,), (0,)), ((), ())),
            preferred_element_type=jnp.float32,
        ).astype(jnp.bfloat16)
        returns[s].start()
        term = jnp.dot(whole, block_j[s], preferred_element_type=jnp.float32)
        for r in range(rows):
            add_row(gamma_alpha, s == 0, r, row_i[s], term)

    for s in each:
        sums(s)
        if s >= 1:
            forward(s - 1)
        crossing(s)
        if s >= 1:
            terms(s - 1)
        amplitude(s)
    forward(slots - 1)
    terms(slots - 1)
    stores = [
        pltpu.make_async_copy(src.at[r], dst.at[r], out_sems.at[n, r])
        for n, (src, dst) in enumerate(
            [(gamma_alpha, gamma_alpha_hbm), (gamma_beta, gamma_beta_hbm)]
        )
        for r in range(rows)
    ]
    for r in range(rows):
        stores[r].start()
    for s in each:
        returns[s].wait_recv()
        for r in range(rows):
            add_row(gamma_beta, s == 0, r, row_out[s], term_recv[s].astype(jnp.float32))
            if s == slots - 1:
                stores[rows + r].start()
    for s in each:
        for copy in [fetches[s], halves[s], nears[s], returns[s]]:
            copy.wait_send()
        for copy in crosses[s] + fars[s] + forwards[s]:
            copy.wait_send()
    for store in stores:
        store.wait()


def solution(mesh):
    workers, parts = mesh.shape["occ"], mesh.shape["aux"]

    def shards(
        b_alpha,
        b_beta,
        eps_occ_alpha,
        eps_occ_beta,
        eps_vir_alpha,
        eps_vir_beta,
        row_orbital,
        pair_list,
        live_mask,
    ):
        rows, nvir, cols = b_alpha.shape
        slots = pair_list.shape[0]
        quarter = nvir // parts
        chips = parts // 2
        hbm = pl.BlockSpec(memory_space=pltpu.HBM)
        gamma = jax.ShapeDtypeStruct((rows, nvir, cols), jnp.float32)
        block = pltpu.VMEM((slots, nvir, cols), jnp.bfloat16)
        piece = (quarter, nvir)
        copies = pltpu.SemaphoreType.DMA((2, slots))
        hop_copies = pltpu.SemaphoreType.DMA((2, slots, chips - 1))
        pairs = jnp.transpose(pair_list, (0, 2, 1))
        return pl.pallas_call(
            functools.partial(kernel, workers, parts, slots),
            out_shape=(gamma, gamma),
            in_specs=[hbm] * 9,
            out_specs=(hbm, hbm),
            scratch_shapes=[
                pltpu.VMEM(b_alpha.shape, b_alpha.dtype),
                pltpu.VMEM(b_beta.shape, b_beta.dtype),
                pltpu.VMEM((parts, quarter), jnp.float32),
                pltpu.VMEM((1, nvir), jnp.float32),
                pltpu.SMEM(eps_occ_alpha.shape, jnp.float32),
                pltpu.SMEM(eps_occ_beta.shape, jnp.float32),
                pltpu.SMEM(row_orbital.shape, jnp.int32),
                pltpu.SMEM(pairs.shape, jnp.int32),
                pltpu.SMEM(live_mask.shape, jnp.int32),
                pltpu.VMEM(gamma.shape, jnp.float32),
                pltpu.VMEM(gamma.shape, jnp.float32),
                block,
                block,
                pltpu.VMEM((slots, 2, chips) + piece, jnp.bfloat16),
                pltpu.VMEM((slots, chips) + piece, jnp.bfloat16),
                pltpu.VMEM((slots, chips - 1) + piece, jnp.bfloat16),
                pltpu.VMEM((slots, chips - 1) + piece, jnp.bfloat16),
                pltpu.VMEM((slots, 2, chips) + piece, jnp.bfloat16),
                block,
                block,
                pltpu.SemaphoreType.DMA((9,)),
                pltpu.SemaphoreType.DMA((2, rows)),
                copies,
                copies,
                hop_copies,
                copies,
                hop_copies,
                hop_copies,
                copies,
            ],
            compiler_params=pltpu.CompilerParams(
                collective_id=0, has_side_effects=True, vmem_limit_bytes=56 * 1024 * 1024
            ),
        )(
            b_alpha,
            b_beta,
            eps_vir_alpha.reshape(parts, quarter),
            eps_vir_beta.reshape(1, nvir),
            eps_occ_alpha,
            eps_occ_beta,
            row_orbital,
            pairs,
            live_mask,
        )

    placed = (P("occ", None, "aux"), P("occ", None, "aux"), P(), P(), P(), P(), P(), P(), P())
    return jax.shard_map(
        shards,
        mesh=mesh,
        in_specs=placed,
        out_specs=(P("occ", None, "aux"), P("occ", None, "aux")),
        check_vma=False,
    )
```

```python
import functools

import jax
import jax.numpy as jnp
from jax import lax
from jax.experimental import pallas as pl
from jax.experimental.pallas import tpu as pltpu
from jax.sharding import PartitionSpec as P

MESH = pl.DeviceIdType.MESH


def kernel(
    workers,
    parts,
    slots,
    chunks,
    b_alpha_hbm,
    b_beta_hbm,
    vir_alpha_hbm,
    vir_beta_hbm,
    occ_alpha_hbm,
    occ_beta_hbm,
    row_orbital_hbm,
    pair_list_hbm,
    live_mask_hbm,
    gamma_alpha,
    gamma_beta,
    b_alpha,
    b_beta,
    eps_vir_alpha,
    eps_vir_beta,
    eps_occ_alpha,
    eps_occ_beta,
    row_orbital,
    pair_list,
    live_mask,
    send_block,
    block_j,
    half_send,
    half_recv,
    cross_send,
    cross_recv,
    amp,
    term_send,
    term_recv,
    in_sems,
    fetch_sems,
    half_sems,
    cross_sems,
    pair_sems,
    far_sems,
    forward_sems,
    term_sems,
):
    rows, nvir, cols = b_alpha.shape
    chips = parts // 2
    quarter = nvir // parts
    width = nvir // chunks
    worker = lax.axis_index("occ")
    me = lax.axis_index("aux")
    chip, core = me // 2, lax.rem(me, 2)
    partner = me + 1 - 2 * core
    distances = [1 + s * (workers // slots) for s in range(slots)]
    ahead = [lax.rem(worker + d, workers) for d in distances]
    behind = [lax.rem(worker + workers - d, workers) for d in distances]
    others = [lax.rem(chip + k, chips) for k in range(1, chips)]
    sources = [lax.rem(chip + chips - k, chips) for k in range(1, chips)]

    loads = [
        pltpu.make_async_copy(src, dst, in_sems.at[n])
        for n, (src, dst) in enumerate(
            [
                (b_beta_hbm, b_beta),
                (row_orbital_hbm, row_orbital),
                (pair_list_hbm, pair_list),
                (live_mask_hbm, live_mask),
                (occ_alpha_hbm, eps_occ_alpha),
                (occ_beta_hbm, eps_occ_beta),
                (vir_alpha_hbm, eps_vir_alpha),
                (vir_beta_hbm, eps_vir_beta),
                (b_alpha_hbm, b_alpha),
            ]
        )
    ]
    for load in loads:
        load.start()
    barrier = pltpu.get_barrier_semaphore()
    for target in ahead + behind:
        pl.semaphore_signal(barrier, inc=1, device_id={"occ": target}, device_id_type=MESH)
    for peer in [partner] + [other * 2 + core for other in others]:
        pl.semaphore_signal(barrier, inc=1, device_id={"aux": peer}, device_id_type=MESH)
    for load in loads[:3]:
        load.wait()

    def local_row(label):
        found = jnp.int32(0)
        for r in range(rows):
            found = jnp.where(row_orbital[worker * rows + r] == label, r, found)
        return found

    row_i = [local_row(pair_list[s, 0, worker]) for s in range(slots)]
    row_out = [local_row(pair_list[s, 1, ahead[s]]) for s in range(slots)]
    for s in range(slots):
        send_block[s] = b_beta[row_out[s]]
    pl.semaphore_wait(barrier, 2 * slots + chips)

    def remote(src, dst, sems, index, where):
        return pltpu.make_async_remote_copy(
            src_ref=src,
            dst_ref=dst,
            send_sem=sems.at[(0,) + index],
            recv_sem=sems.at[(1,) + index],
            device_id=where,
            device_id_type=MESH,
        )

    each = range(slots)
    hops = range(chips - 1)
    steps = range(chunks)
    spans = [pl.ds(c * width, width) for c in steps]
    fetches = [
        [
            remote(
                send_block.at[s, spans[c]], block_j.at[s, spans[c]], fetch_sems, (c, s),
                {"occ": ahead[s]},
            )
            for s in each
        ]
        for c in steps
    ]
    halves = [
        remote(half_send.at[c, 1 - core], half_recv.at[c], half_sems, (c,), {"aux": partner})
        for c in steps
    ]
    crosses = [
        [
            remote(
                cross_send.at[c, k], cross_recv.at[c, k], cross_sems, (c, k),
                {"aux": others[k] * 2 + core},
            )
            for k in hops
        ]
        for c in steps
    ]
    nears = [
        remote(amp.at[c, core, chip], amp.at[c, core, chip], pair_sems, (c,), {"aux": partner})
        for c in steps
    ]
    fars = [
        [
            remote(
                amp.at[c, core, chip], amp.at[c, core, chip], far_sems, (c, k),
                {"aux": others[k] * 2 + core},
            )
            for k in hops
        ]
        for c in steps
    ]
    forwards = [
        [
            remote(
                amp.at[c, core, sources[k]], amp.at[c, core, sources[k]], forward_sems, (c, k),
                {"aux": partner},
            )
            for k in hops
        ]
        for c in steps
    ]
    returns = [
        [
            remote(
                term_send.at[s, spans[c]], term_recv.at[s, spans[c]], term_sems, (c, s),
                {"occ": behind[s]},
            )
            for s in each
        ]
        for c in steps
    ]
    for c in steps:
        for s in each:
            fetches[c][s].start()
    for load in loads[3:]:
        load.wait()

    vir_row = eps_vir_alpha[pl.ds(core * chips + chip, 1), :]
    vir_column = jnp.broadcast_to(vir_row, (quarter, quarter)).T[:, :1]

    def sums(c):
        for s in each:
            fetches[c][s].wait_recv()
            partial = lax.dot_general(
                b_alpha[row_i[s]],
                block_j[s, spans[c]],
                (((1,), (1,)), ((), ())),
                preferred_element_type=jnp.float32,
            )
            half_send[c, :, :, s] = partial.astype(jnp.bfloat16).reshape(2, chips, quarter, width)
        halves[c].start()

    def pair_sum(c, owner):
        return half_send[c, core, owner].astype(jnp.float32) + half_recv[c, owner].astype(jnp.float32)

    def crossing(c):
        halves[c].wait_recv()
        for k in hops:
            cross_send[c, k] = pair_sum(c, others[k]).astype(jnp.bfloat16)
            crosses[c][k].start()

    def amplitude(c):
        total = pair_sum(c, chip)
        for k in hops:
            crosses[c][k].wait_recv()
            total = total + cross_recv[c, k].astype(jnp.float32)
        gap = vir_column + eps_vir_beta[:, spans[c]]
        for s in each:
            occ_alpha = eps_occ_alpha[pair_list[s, 0, worker]]
            occ_beta = eps_occ_beta[pair_list[s, 1, worker]]
            live = live_mask[s, worker].astype(jnp.float32)
            value = live * total[s] / (gap - occ_alpha - occ_beta)
            amp[c, core, chip, s] = value.astype(jnp.bfloat16)
        for copy in fars[c]:
            copy.start()
        nears[c].start()

    def forward(c):
        for k in hops:
            fars[c][k].wait_recv()
            forwards[c][k].start()

    def terms(c):
        nears[c].wait_recv()
        for copy in forwards[c]:
            copy.wait_recv()
        for s in each:
            term_send[s, spans[c]] = lax.dot_general(
                amp[c, :, :, s].reshape(nvir, width),
                b_alpha[row_i[s]],
                (((0,), (0,)), ((), ())),
                preferred_element_type=jnp.float32,
            ).astype(jnp.bfloat16)
            returns[c][s].start()

    for c in steps:
        sums(c)
        if c >= 1:
            forward(c - 1)
        crossing(c)
        if c >= 1:
            terms(c - 1)
        amplitude(c)
    forward(chunks - 1)
    terms(chunks - 1)
    for s in each:
        whole = jnp.concatenate([amp[c, :, :, s].reshape(nvir, width) for c in steps], axis=1)
        term = jnp.dot(whole, block_j[s], preferred_element_type=jnp.float32)
        for r in range(rows):
            share = jnp.where(row_i[s] == r, term, 0.0)
            gamma_alpha[r] = share if s == 0 else gamma_alpha[r] + share
    for c in steps:
        for s in each:
            returns[c][s].wait_recv()
        for r in range(rows):
            total = jnp.where(row_out[0] == r, term_recv[0, spans[c]].astype(jnp.float32), 0.0)
            for s in range(1, slots):
                total = total + jnp.where(
                    row_out[s] == r, term_recv[s, spans[c]].astype(jnp.float32), 0.0
                )
            gamma_beta[r, spans[c]] = total
    for c in steps:
        for copy in fetches[c] + [halves[c], nears[c]] + returns[c]:
            copy.wait_send()
        for copy in crosses[c] + fars[c] + forwards[c]:
            copy.wait_send()


def solution(mesh):
    workers, parts = mesh.shape["occ"], mesh.shape["aux"]

    def shards(
        b_alpha,
        b_beta,
        eps_occ_alpha,
        eps_occ_beta,
        eps_vir_alpha,
        eps_vir_beta,
        row_orbital,
        pair_list,
        live_mask,
    ):
        rows, nvir, cols = b_alpha.shape
        slots = pair_list.shape[0]
        quarter = nvir // parts
        chips = parts // 2
        vmem = pl.BlockSpec(memory_space=pltpu.VMEM)
        hbm = pl.BlockSpec(memory_space=pltpu.HBM)
        gamma = jax.ShapeDtypeStruct((rows, nvir, cols), jnp.float32)
        block = pltpu.VMEM((slots, nvir, cols), jnp.bfloat16)
        chunks = max(1, nvir // 128)
        piece = (slots, quarter, nvir // chunks)
        block_copies = pltpu.SemaphoreType.DMA((2, chunks, slots))
        copies = pltpu.SemaphoreType.DMA((2, chunks))
        hop_copies = pltpu.SemaphoreType.DMA((2, chunks, chips - 1))
        pairs = jnp.transpose(pair_list, (0, 2, 1))
        return pl.pallas_call(
            functools.partial(kernel, workers, parts, slots, chunks),
            out_shape=(gamma, gamma),
            in_specs=[hbm] * 9,
            out_specs=(vmem, vmem),
            scratch_shapes=[
                pltpu.VMEM(b_alpha.shape, b_alpha.dtype),
                pltpu.VMEM(b_beta.shape, b_beta.dtype),
                pltpu.VMEM((parts, quarter), jnp.float32),
                pltpu.VMEM((1, nvir), jnp.float32),
                pltpu.SMEM(eps_occ_alpha.shape, jnp.float32),
                pltpu.SMEM(eps_occ_beta.shape, jnp.float32),
                pltpu.SMEM(row_orbital.shape, jnp.int32),
                pltpu.SMEM(pairs.shape, jnp.int32),
                pltpu.SMEM(live_mask.shape, jnp.int32),
                block,
                block,
                pltpu.VMEM((chunks, 2, chips) + piece, jnp.bfloat16),
                pltpu.VMEM((chunks, chips) + piece, jnp.bfloat16),
                pltpu.VMEM((chunks, chips - 1) + piece, jnp.bfloat16),
                pltpu.VMEM((chunks, chips - 1) + piece, jnp.bfloat16),
                pltpu.VMEM((chunks, 2, chips) + piece, jnp.bfloat16),
                block,
                block,
                pltpu.SemaphoreType.DMA((9,)),
                block_copies,
                copies,
                hop_copies,
                copies,
                hop_copies,
                hop_copies,
                block_copies,
            ],
            compiler_params=pltpu.CompilerParams(
                collective_id=0, has_side_effects=True, vmem_limit_bytes=56 * 1024 * 1024
            ),
        )(
            b_alpha,
            b_beta,
            eps_vir_alpha.reshape(parts, quarter),
            eps_vir_beta.reshape(1, nvir),
            eps_occ_alpha,
            eps_occ_beta,
            row_orbital,
            pairs,
            live_mask,
        )

    placed = (P("occ", None, "aux"), P("occ", None, "aux"), P(), P(), P(), P(), P(), P(), P())
    return jax.shard_map(
        shards,
        mesh=mesh,
        in_specs=placed,
        out_specs=(P("occ", None, "aux"), P("occ", None, "aux")),
        check_vma=False,
    )
```
